32 devices in a mesh: head: 4 (over y, x), seq: 8 (over z, core).
Axes of the slice: x: 2, y: 2, z: 4, core: 2. Of those that a mesh axis runs over, the one named last changes fastest.
Arguments:
- queries: bfloat16 [8, 64, 576], P('seq', 'head'), may hold values from -400 to 400
- query_pos: int32 [8], replicated, may hold values from 2019 to 2047, as said below
- latents: bfloat16 [2048, 576], P('seq'), may hold values from -6 to 6
- valid_keys: int32 [8], P('seq'), may hold values from 128 to 256, as said below
- output_gradient: bfloat16 [8, 64, 512], P('seq', 'head'), may hold values from -600 to 600
- kv_down: bfloat16 [7168, 576], P('head'), may hold values from -0.0625 to 0.0625
Outputs:
- latent_grad: float32 [2048, 576], P('seq')
- input_grad: bfloat16 [2048, 7168], P('seq', 'head')
The draws below stay inside these ranges and needn't reach their ends.
Inputs may be any that keep to these rules, and one draw needn't show every extreme that they name: `query_pos`: positions rise strictly with the query index, consecutive ones differ by 1 to 4, and the last is 2047. The first valid_keys[s] positions of shard s are valid; some shard is full and some holds exactly half.
All inputs are finite; a program needn't handle non-finite values.
Results may differ from the reference program's by a relative error of at most 0.015.
Values may be sent and summed in bfloat16 or wider, within the bound.
No kernel may reach another device: no remote copies, remote signals or barrier semaphores. Data moves between devices by JAX's collectives and lax.ppermute only.
A program may use at most 64 MiB of HBM per device.

```python
import jax
import jax.numpy as jnp
from jax import lax

D = 7168
LATENT_WIDTH = 512
HEADS_DEV = 16
SHARD_KEY_COUNT = 256
LAT = 576
HEAD_TOTAL = 64
S = 2048
QUERY_TOTAL = 8


def sign_pattern(key):
    raw = jax.random.normal(jax.random.fold_in(key, 31), (LAT,), jnp.float32)
    return jnp.where(raw > 0.0, 2.0, -2.0)


def shared_latents(key):
    offset_start = jax.random.normal(jax.random.fold_in(key, 11), (S, LAT), jnp.float32)
    offset_start = jnp.clip(offset_start, -6.0, 6.0)
    pattern = sign_pattern(key)
    offset_start = offset_start.at[0, :].set(pattern)
    offset_start = offset_start.at[SHARD_KEY_COUNT, :].set(pattern * (1.0 - 2.0 / 360.0))
    return offset_start


def draw_latents(key, part):
    return shared_latents(key).astype(jnp.bfloat16)


def draw_queries(key, part):
    pattern = sign_pattern(key)
    value_rows = jax.random.normal(jax.random.fold_in(key, 13), (QUERY_TOTAL, HEAD_TOTAL, LAT), jnp.float32)
    value_rows = jnp.clip(value_rows, -6.0, 6.0)
    unit = 1.0 / (192.0 ** (-0.5) * 4.0 * LAT)
    for cache_position, target_score in enumerate((120.0, 240.0, 360.0)):
        value_rows = value_rows.at[cache_position, 0, :].set(target_score * unit * pattern)
    return value_rows.astype(jnp.bfloat16)


def draw_query_pos(key, part):
    spacing = jax.random.randint(jax.random.fold_in(key, 17), (QUERY_TOTAL,), 1, 5, jnp.int32)
    after = jnp.cumsum(spacing[::-1])[::-1] - spacing
    return (S - 1 - after).astype(jnp.int32)


def draw_valid_keys(key, part):
    shard_total = S // SHARD_KEY_COUNT
    counts = jax.random.randint(jax.random.fold_in(key, 23), (shard_total,), SHARD_KEY_COUNT // 2, SHARD_KEY_COUNT + 1, jnp.int32)
    order = jax.random.permutation(jax.random.fold_in(key, 29), shard_total)
    counts = counts.at[order[0]].set(SHARD_KEY_COUNT)
    counts = counts.at[order[1]].set(SHARD_KEY_COUNT // 2)
    return counts.astype(jnp.int32)


def block_levels(rng, shape, split, least, top_value):
    gain, own = 1.0, jax.random.fold_in(rng, 6)
    for position, blocks in split:
        steps = jnp.exp(jax.random.uniform(jax.random.fold_in(own, position), (blocks,), jnp.float32, least / len(split), top_value / len(split)))
        gain = gain * jnp.repeat(steps, shape[position] // blocks).reshape([-1 if axis == position else 1 for axis in range(len(shape))])
    return gain


def noise(stream_key, extent, width, most, split=(), kind=jnp.bfloat16):
    loudness = block_levels(stream_key, extent, split, -0.22, 0.18) if split else 1.0
    entries = jax.random.normal(stream_key, extent, jnp.float32) * width * loudness
    return jnp.minimum(jnp.maximum(entries, -most), most).astype(kind)


def setup_inputs(seed: int = 0) -> dict:
    arg_keys = jax.random.split(jax.random.key(seed), 7)
    queries = draw_queries(jax.random.fold_in(arg_keys[6], 71), 0)
    query_pos = draw_query_pos(jax.random.fold_in(arg_keys[6], 71), 0)
    latents = draw_latents(jax.random.fold_in(arg_keys[6], 71), 0)
    valid_keys = draw_valid_keys(jax.random.fold_in(arg_keys[6], 71), 0)
    output_gradient = noise(arg_keys[4], (QUERY_TOTAL, HEAD_TOTAL, LATENT_WIDTH), 100.0, 600.0, ((0, 8), (1, 4)))
    kv_down = noise(arg_keys[5], (D, LAT), D ** -0.5, 0.0625, ((0, 4),))
    return dict(queries=queries, query_pos=query_pos, latents=latents, valid_keys=valid_keys, output_gradient=output_gradient, kv_down=kv_down)


score_scale = 192.0 ** -0.5


def reference(queries, query_pos, latents, valid_keys, output_gradient, kv_down):
    total_keys = latents.shape[0]
    key_pos = jnp.arange(total_keys, dtype=jnp.int32)
    shard_index = key_pos // SHARD_KEY_COUNT
    local_index = key_pos % SHARD_KEY_COUNT
    key_valid = local_index < valid_keys[shard_index]
    visible = key_valid[None, :] & (key_pos[None, :] <= query_pos[:, None])
    keys_wide = latents.astype(jnp.float32)
    value_rows = latents[:, :LATENT_WIDTH].astype(jnp.float32)
    group_count = queries.shape[1] // HEADS_DEV

    def one_group(running, group):
        first_head = (group * HEADS_DEV).astype(jnp.int32)
        block_query = lax.dynamic_slice_in_dim(queries, first_head, HEADS_DEV, 1).astype(jnp.float32)
        block_grad = lax.dynamic_slice_in_dim(output_gradient, first_head, HEADS_DEV, 1).astype(jnp.float32)
        scores = jnp.einsum("qhc,kc->qhk", block_query, keys_wide) * score_scale
        scores = jnp.where(visible[:, None, :], scores, -jnp.inf)
        row_max = jnp.max(scores, axis=-1, keepdims=True)
        lse = row_max + jnp.log(jnp.sum(jnp.exp(scores - row_max), axis=-1, keepdims=True))
        probs = jnp.exp(scores - lse)
        dprobs = jnp.einsum("mcg,dg->mcd", block_grad, value_rows)
        delta_rows = jnp.sum(probs * dprobs, axis=-1, keepdims=True)
        dscores = probs * (dprobs - delta_rows)
        probs_b = lax.optimization_barrier(probs.astype(jnp.bfloat16)).astype(jnp.float32)
        dscores_b = lax.optimization_barrier(dscores.astype(jnp.bfloat16)).astype(jnp.float32)
        key_contribution = jnp.einsum("qhk,qhc->kc", dscores_b, block_query) * score_scale
        value_contribution = jnp.einsum("qhk,qhv->kv", probs_b, block_grad)
        partial_product = jnp.concatenate([key_contribution[:, :LATENT_WIDTH] + value_contribution, key_contribution[:, LATENT_WIDTH:]], axis=1)
        return running + partial_product, None

    latent_grad, _ = lax.scan(one_group, jnp.zeros((total_keys, LAT), jnp.float32), jnp.arange(group_count, dtype=jnp.int32))
    input_grad = lax.dot_general(latent_grad.astype(jnp.bfloat16), kv_down, (((1,), (1,)), ((), ())), preferred_element_type=jnp.float32).astype(jnp.bfloat16)
    return latent_grad, input_grad
```

```python
import functools

import jax
import jax.numpy as jnp
from jax import lax
from jax.experimental import pallas as pl
from jax.experimental.pallas import tpu as pltpu
from jax.sharding import PartitionSpec as P

score_scale = 192.0 ** (-0.5)
hidden = -1e30
row_tile = 128
stat_rows = 8


VMEM = pl.BlockSpec(memory_space=pltpu.VMEM)
SMEM = pl.BlockSpec(memory_space=pltpu.SMEM)


def swap(value, axis, size, bit):
    return lax.ppermute(value, axis, [(i, i ^ bit) for i in range(size)])


def bits_of(size):
    assert size & (size - 1) == 0, "axis size"
    return [1 << i for i in range(size.bit_length() - 1)]


def gathered_rows(own, axis, size):
    held = [(own, [0])]
    for bit in reversed(bits_of(size)):
        if len(held) > 2:
            held = [(jnp.concatenate([h for h, _ in held], 0), sum([o for _, o in held], []))]
        held = held + [(swap(h, axis, size, bit), [o ^ bit for o in offs]) for h, offs in held]
    return held


def scores_kernel(offsets, own_rows, heads, here, query_pos, valid, *refs):
    pieces, (lat,) = refs[: len(offsets)], refs[len(offsets) : len(offsets) + 1]
    rows, e_out, dp_out, stats = refs[len(offsets) + 1 :]
    total_rows, keys = e_out.shape
    width = lat.shape[0]
    span = rows.shape[1] - width
    me, first_key = here[0], here[0] * keys
    for piece, offs in zip(pieces, offsets):
        for j, off in enumerate(offs):
            start = pl.multiple_of((me ^ off) * own_rows, own_rows)
            rows[pl.ds(start, own_rows), :] = piece[j * own_rows : (j + 1) * own_rows, :]
    tile = min(row_tile, total_rows)

    def step(t, carry):
        start = pl.multiple_of(t * tile, tile)
        block = rows[pl.ds(start, tile), :]
        s = jnp.dot(block[:, :width], lat[...], preferred_element_type=jnp.float32) * score_scale
        dp = jnp.dot(block[:, width:], lat[:span, :], preferred_element_type=jnp.float32)
        index = lax.broadcasted_iota(jnp.int32, (heads, keys), 1)
        masked = []
        for i in range(tile // heads):
            limit = jnp.minimum(query_pos[t * (tile // heads) + i] - first_key, valid[0] - 1)
            masked.append(jnp.where(index <= limit, s[i * heads : (i + 1) * heads], hidden))
        s = jnp.concatenate(masked, 0)
        top = jnp.max(s, axis=1, keepdims=True)
        e = jnp.exp(s - top)
        e_out[pl.ds(start, tile), :] = e
        dp_out[pl.ds(start, tile), :] = dp
        total = jnp.sum(e, axis=1, keepdims=True)
        weighted = jnp.sum(e * dp, axis=1, keepdims=True)
        lane = lax.broadcasted_iota(jnp.int32, (tile, 128), 1)
        packed = jnp.where(lane == 0, top, jnp.where(lane == 1, total, weighted))
        stats[:, pl.ds(start, tile)] = packed.T[:stat_rows, :]
        return carry

    lax.fori_loop(0, total_rows // tile, step, 0)


def join(a, b):
    top = jnp.maximum(a[0:1], b[0:1])
    wa, wb = jnp.exp(a[0:1] - top), jnp.exp(b[0:1] - top)
    return top, a[1:2] * wa + b[1:2] * wb, a[2:3] * wa + b[2:3] * wb


def join_kernel(a, b, out):
    top, total, weighted = join(a[...], b[...])
    out[...] = jnp.concatenate([top, total, jnp.broadcast_to(weighted, (stat_rows - 2, top.shape[1]))], 0)


def grads_kernel(rows, e_in, dp_in, own, a, b, *outs):
    total_rows, keys = e_in.shape
    width = outs[0].shape[0] if len(outs) == 2 else None
    span = rows.shape[1] - width
    tile = min(row_tile, total_rows)
    half = keys // 2

    def part(t):
        start = pl.multiple_of(t * tile, tile)
        lanes = pl.ds(start, tile)
        top, total, weighted = join(a[:, lanes], b[:, lanes])
        lse = top + jnp.log(total)
        factor = jnp.exp(own[0:1, lanes] - lse)
        delta = weighted / total
        pair = jnp.concatenate([factor, jnp.broadcast_to(delta, (tile - 1, tile))], 0).T
        probs = e_in[lanes, :] * pair[:, 0:1]
        dscores = (probs * (dp_in[lanes, :] - pair[:, 1:2])).astype(jnp.bfloat16)
        probs = probs.astype(jnp.bfloat16)
        block = rows[lanes, :]
        dims = (((0,), (0,)), ((), ()))
        key = lax.dot_general(block[:, :width], dscores, dims, preferred_element_type=jnp.float32) * score_scale
        value = lax.dot_general(block[:, width:], probs, dims, preferred_element_type=jnp.float32)
        return jnp.concatenate([key[:span] + value, key[span:]], 0)

    steps = total_rows // tile
    if steps == 1:
        result = part(0)
    else:
        result = lax.fori_loop(0, steps, lambda t, c: c + part(t), jnp.zeros((width, keys), jnp.float32))
    outs[0][...] = result[:, :half].astype(jnp.bfloat16)
    outs[1][...] = result[:, half:].astype(jnp.bfloat16)


def shards(sizes, queries, query_pos, latents, valid_keys, output_gradient, kv_down):
    seq, head = sizes["seq"], sizes["head"]
    keys, width = latents.shape
    span = output_gradient.shape[2]
    heads = queries.shape[1]
    own_rows = queries.shape[0] * heads
    total_rows = own_rows * seq
    f32, bf16 = jnp.float32, jnp.bfloat16
    lat = latents.T
    here = lax.axis_index("seq").astype(jnp.int32).reshape(1)

    own = jnp.concatenate([queries.reshape(own_rows, width), output_gradient.reshape(own_rows, span)], 1)
    pieces = gathered_rows(own, "seq", seq)
    rows, e, dp, stats = pl.pallas_call(
        functools.partial(scores_kernel, [o for _, o in pieces], own_rows, heads),
        out_shape=(
            jax.ShapeDtypeStruct((total_rows, width + span), bf16),
            jax.ShapeDtypeStruct((total_rows, keys), f32),
            jax.ShapeDtypeStruct((total_rows, keys), f32),
            jax.ShapeDtypeStruct((stat_rows, total_rows), f32),
        ),
        in_specs=[SMEM, SMEM, SMEM] + [VMEM] * (len(pieces) + 1),
        out_specs=(VMEM,) * 4,
        name="scores",
    )(here, query_pos, valid_keys, *[p for p, _ in pieces], lat)

    joined, bits = stats, bits_of(seq)
    other = swap(joined, "seq", seq, bits[0])
    for bit in bits[1:]:
        joined = pl.pallas_call(
            join_kernel,
            out_shape=jax.ShapeDtypeStruct(stats.shape, f32),
            in_specs=[VMEM, VMEM],
            out_specs=VMEM,
            name="join",
        )(joined, other)
        other = swap(joined, "seq", seq, bit)

    halves = pl.pallas_call(
        grads_kernel,
        out_shape=(jax.ShapeDtypeStruct((width, keys // 2), bf16),) * 2,
        in_specs=[VMEM] * 6,
        out_specs=(VMEM,) * 2,
        name="grads",
    )(rows, e, dp, stats, joined, other)

    orders = (bits_of(head), bits_of(head)[::-1])
    halves = list(halves)
    for step in range(len(orders[0])):
        received = [swap(h, "head", head, order[step]) for h, order in zip(halves, orders)]
        halves = [h.astype(f32) + r.astype(f32) for h, r in zip(halves, received)]
        if step < len(orders[0]) - 1:
            halves = [h.astype(bf16) for h in halves]
    grad = jnp.concatenate(halves, 1)
    input_grad = lax.dot_general(
        grad.astype(bf16), kv_down, (((0,), (1,)), ((), ())), preferred_element_type=f32
    ).astype(bf16)
    return grad.T, input_grad


def solution(mesh):
    placed = (
        P("seq", "head", None),
        P(),
        P("seq", None),
        P("seq"),
        P("seq", "head", None),
        P("head", None),
    )
    return jax.shard_map(
        functools.partial(shards, dict(mesh.shape)),
        mesh=mesh,
        in_specs=placed,
        out_specs=(P("seq", None), P("seq", "head")),
        check_vma=False,
    )
```

```python
import functools

import jax
import jax.numpy as jnp
from jax import lax
from jax.experimental import pallas as pl
from jax.experimental.pallas import tpu as pltpu
from jax.sharding import PartitionSpec as P

score_scale = 192.0 ** (-0.5)
hidden = -1e30
row_tile = 128
stat_rows = 8


VMEM = pl.BlockSpec(memory_space=pltpu.VMEM)
SMEM = pl.BlockSpec(memory_space=pltpu.SMEM)


def room(*arrays):
    held = sum(a.size * a.dtype.itemsize for a in arrays)
    return pltpu.CompilerParams(vmem_limit_bytes=min(3 * held + (4 << 20), 60 << 20))


def swap(value, axis, size, bit):
    return lax.ppermute(value, axis, [(i, i ^ bit) for i in range(size)])


def bits_of(size):
    assert size & (size - 1) == 0, "axis size"
    return [1 << i for i in range(size.bit_length() - 1)]


def gathered_rows(own, axis, size):
    held = [(own, [0])]
    for bit in reversed(bits_of(size)):
        if len(held) > 2:
            held = [(jnp.concatenate([h for h, _ in held], 0), sum([o for _, o in held], []))]
        held = held + [(swap(h, axis, size, bit), [o ^ bit for o in offs]) for h, offs in held]
    return held


def scores_kernel(offsets, own_rows, heads, here, query_pos, valid, *refs):
    pieces, (lat,) = refs[: len(offsets)], refs[len(offsets) : len(offsets) + 1]
    rows, e_out, dp_out, stats = refs[len(offsets) + 1 :]
    total_rows, keys = e_out.shape
    width = lat.shape[0]
    span = rows.shape[1] - width
    me, first_key = here[0], here[0] * keys
    for piece, offs in zip(pieces, offsets):
        for j, off in enumerate(offs):
            start = pl.multiple_of((me ^ off) * own_rows, own_rows)
            rows[pl.ds(start, own_rows), :] = piece[j * own_rows : (j + 1) * own_rows, :]
    tile = min(row_tile, total_rows)

    def step(t, carry):
        start = pl.multiple_of(t * tile, tile)
        block = rows[pl.ds(start, tile), :]
        s = jnp.dot(block[:, :width], lat[...], preferred_element_type=jnp.float32) * score_scale
        dp = jnp.dot(block[:, width:], lat[:span, :], preferred_element_type=jnp.float32)
        index = lax.broadcasted_iota(jnp.int32, (heads, keys), 1)
        masked = []
        for i in range(tile // heads):
            limit = jnp.minimum(query_pos[t * (tile // heads) + i] - first_key, valid[0] - 1)
            masked.append(jnp.where(index <= limit, s[i * heads : (i + 1) * heads], hidden))
        s = jnp.concatenate(masked, 0)
        top = jnp.max(s, axis=1, keepdims=True)
        e = jnp.exp(s - top)
        e_out[pl.ds(start, tile), :] = e
        dp_out[pl.ds(start, tile), :] = dp
        total = jnp.sum(e, axis=1, keepdims=True)
        weighted = jnp.sum(e * dp, axis=1, keepdims=True)
        lane = lax.broadcasted_iota(jnp.int32, (tile, 128), 1)
        packed = jnp.where(lane == 0, top, jnp.where(lane == 1, total, weighted))
        stats[:, pl.ds(start, tile)] = packed.T[:stat_rows, :]
        return carry

    lax.fori_loop(0, total_rows // tile, step, 0)


def join(a, b):
    top = jnp.maximum(a[0:1], b[0:1])
    wa, wb = jnp.exp(a[0:1] - top), jnp.exp(b[0:1] - top)
    return top, a[1:2] * wa + b[1:2] * wb, a[2:3] * wa + b[2:3] * wb


def join_kernel(a, b, out):
    top, total, weighted = join(a[...], b[...])
    out[...] = jnp.concatenate([top, total, jnp.broadcast_to(weighted, (stat_rows - 2, top.shape[1]))], 0)


def grads_kernel(rows, e_in, dp_in, own, a, b, *outs):
    total_rows, keys = e_in.shape
    width = outs[0].shape[0] if len(outs) == 2 else None
    span = rows.shape[1] - width
    tile = min(row_tile, total_rows)
    half = keys // 2

    def part(t):
        start = pl.multiple_of(t * tile, tile)
        lanes = pl.ds(start, tile)
        top, total, weighted = join(a[:, lanes], b[:, lanes])
        lse = top + jnp.log(total)
        factor = jnp.exp(own[0:1, lanes] - lse)
        delta = weighted / total
        pair = jnp.concatenate([factor, jnp.broadcast_to(delta, (tile - 1, tile))], 0).T
        probs = e_in[lanes, :] * pair[:, 0:1]
        dscores = (probs * (dp_in[lanes, :] - pair[:, 1:2])).astype(jnp.bfloat16)
        probs = probs.astype(jnp.bfloat16)
        block = rows[lanes, :]
        dims = (((0,), (0,)), ((), ()))
        key = lax.dot_general(block[:, :width], dscores, dims, preferred_element_type=jnp.float32) * score_scale
        value = lax.dot_general(block[:, width:], probs, dims, preferred_element_type=jnp.float32)
        return jnp.concatenate([key[:span] + value, key[span:]], 0)

    steps = total_rows // tile
    if steps == 1:
        result = part(0)
    else:
        result = lax.fori_loop(0, steps, lambda t, c: c + part(t), jnp.zeros((width, keys), jnp.float32))
    outs[0][...] = result[:, :half].astype(jnp.bfloat16)
    outs[1][...] = result[:, half:].astype(jnp.bfloat16)


def shards(sizes, queries, query_pos, latents, valid_keys, output_gradient, kv_down):
    seq, head = sizes["seq"], sizes["head"]
    keys, width = latents.shape
    span = output_gradient.shape[2]
    heads = queries.shape[1]
    own_rows = queries.shape[0] * heads
    total_rows = own_rows * seq
    f32, bf16 = jnp.float32, jnp.bfloat16
    lat = latents.T
    here = lax.axis_index("seq").astype(jnp.int32).reshape(1)

    own = jnp.concatenate([queries.reshape(own_rows, width), output_gradient.reshape(own_rows, span)], 1)
    pieces = gathered_rows(own, "seq", seq)
    results = (
        jax.ShapeDtypeStruct((total_rows, width + span), bf16),
        jax.ShapeDtypeStruct((total_rows, keys), f32),
        jax.ShapeDtypeStruct((total_rows, keys), f32),
        jax.ShapeDtypeStruct((stat_rows, total_rows), f32),
    )
    rows, e, dp, stats = pl.pallas_call(
        functools.partial(scores_kernel, [o for _, o in pieces], own_rows, heads),
        out_shape=results,
        compiler_params=room(*results),
        in_specs=[SMEM, SMEM, SMEM] + [VMEM] * (len(pieces) + 1),
        out_specs=(VMEM,) * 4,
        name="scores",
    )(here, query_pos, valid_keys, *[p for p, _ in pieces], lat)

    joined, bits = stats, bits_of(seq)
    other = swap(joined, "seq", seq, bits[0])
    for bit in bits[1:]:
        joined = pl.pallas_call(
            join_kernel,
            out_shape=jax.ShapeDtypeStruct(stats.shape, f32),
            compiler_params=room(stats),
            in_specs=[VMEM, VMEM],
            out_specs=VMEM,
            name="join",
        )(joined, other)
        other = swap(joined, "seq", seq, bit)

    halves = pl.pallas_call(
        grads_kernel,
        out_shape=(jax.ShapeDtypeStruct((width, keys // 2), bf16),) * 2,
        in_specs=[VMEM] * 6,
        compiler_params=room(rows, e, dp, stats),
        out_specs=(VMEM,) * 2,
        name="grads",
    )(rows, e, dp, stats, joined, other)

    orders = (bits_of(head), bits_of(head)[::-1])
    halves = list(halves)
    for step in range(len(orders[0])):
        received = [swap(h, "head", head, order[step]) for h, order in zip(halves, orders)]
        halves = [h.astype(f32) + r.astype(f32) for h, r in zip(halves, received)]
        if step < len(orders[0]) - 1:
            halves = [h.astype(bf16) for h in halves]
    grad = jnp.concatenate(halves, 1)
    input_grad = lax.dot_general(
        grad.astype(bf16), kv_down, (((0,), (1,)), ((), ())), preferred_element_type=f32
    ).astype(bf16)
    return grad.T, input_grad


def solution(mesh):
    placed = (
        P("seq", "head", None),
        P(),
        P("seq", None),
        P("seq"),
        P("seq", "head", None),
        P("head", None),
    )
    return jax.shard_map(
        functools.partial(shards, dict(mesh.shape)),
        mesh=mesh,
        in_specs=placed,
        out_specs=(P("seq", None), P("seq", "head")),
        check_vma=False,
    )
```

```python
import functools

import jax
import jax.numpy as jnp
from jax import lax
from jax.experimental import pallas as pl
from jax.experimental.pallas import tpu as pltpu
from jax.sharding import PartitionSpec as P

score_scale = 192.0 ** (-0.5)
hidden, shown = -1e30, 3e38
row_tile = 128
stat_rows = 8
f32, bf16 = jnp.float32, jnp.bfloat16


VMEM = pl.BlockSpec(memory_space=pltpu.VMEM)
SMEM = pl.BlockSpec(memory_space=pltpu.SMEM)
HBM = pl.BlockSpec(memory_space=pl.ANY)


def like(shape, dtype):
    return jax.ShapeDtypeStruct(shape, dtype)


def swap(value, axis, size, bit):
    return lax.ppermute(value, axis, [(i, i ^ bit) for i in range(size)])


def bits_of(size):
    assert size > 1 and size & (size - 1) == 0, "axis size"
    return [1 << i for i in range(size.bit_length() - 1)]


def gathered_rows(own, axis, size, bits):
    held = [(own, [0])]
    for bit in bits:
        if len(held) > 2:
            held = [(jnp.concatenate([h for h, _ in held], 0), sum([o for _, o in held], []))]
        held = held + [(swap(h, axis, size, bit), [o ^ bit for o in offs]) for h, offs in held]
    return [h for h, _ in held], sum([o for _, o in held], [])


def prepare_kernel(offsets, own_rows, heads, here, query_pos, valid, other_valid, lat, other_lat, both, mask):
    keys = lat.shape[1]
    both[:, :keys] = lat[...]
    both[:, keys:] = other_lat[...]
    me, per_device = here[0], own_rows // heads
    index = lax.broadcasted_iota(jnp.int32, (heads, keys), 1)
    for j, off in enumerate(offsets):
        for i in range(per_device):
            rows = slice((j * per_device + i) * heads, (j * per_device + i + 1) * heads)
            position = query_pos[(me ^ off) * per_device + i]
            for part, shard, bound in ((0, me, valid), (1, me ^ 1, other_valid)):
                limit = jnp.minimum(position - shard * keys, bound[0] - 1)
                mask[rows, part * keys : (part + 1) * keys] = jnp.where(index <= limit, shown, hidden)


def scores_kernel(n, *refs):
    pieces, (both, mask, e_out, dp_out, stats) = refs[:n], refs[n:]
    width = both.shape[0]
    span = pieces[0].shape[1] - width
    rows = jnp.concatenate([p[...] for p in pieces], 0)
    packs = []
    for t in range(0, rows.shape[0], row_tile):
        block = rows[t : t + row_tile]
        count = block.shape[0]
        s = jnp.dot(block[:, :width], both[...], preferred_element_type=f32) * score_scale
        s = jnp.minimum(s, mask[t : t + count, :])
        dp = jnp.dot(block[:, width:], both[:span, :], preferred_element_type=f32)
        top = jnp.max(s, axis=1, keepdims=True)
        e = jnp.exp(s - top)
        e_out[t : t + count, :] = e
        dp_out[t : t + count, :] = dp
        total = jnp.sum(e, axis=1, keepdims=True)
        weighted = jnp.sum(e * dp, axis=1, keepdims=True)
        lane = lax.broadcasted_iota(jnp.int32, (count, 128), 1)
        packed = jnp.where(lane == 0, top, jnp.where(lane == 1, total, weighted))
        if count % 128:
            packed = jnp.concatenate([packed, jnp.zeros((128 - count % 128, 128), f32)], 0)
        packs.append(packed.T[:stat_rows, :])
    stats[...] = jnp.concatenate(packs, 1)


def join(a, b, distance):
    lanes = b.shape[1]
    lane = lax.broadcasted_iota(jnp.int32, b.shape, 1)
    b = jnp.where((lane // distance) % 2 == 0, pltpu.roll(b, lanes - distance, 1), pltpu.roll(b, distance, 1))
    top = jnp.maximum(a[0:1], b[0:1])
    wa, wb = jnp.exp(a[0:1] - top), jnp.exp(b[0:1] - top)
    return top, a[1:2] * wa + b[1:2] * wb, a[2:3] * wa + b[2:3] * wb


def join_kernel(distance, a, b, out):
    top, total, weighted = join(a[...], b[...], distance)
    out[...] = jnp.concatenate([top, total, jnp.broadcast_to(weighted, (stat_rows - 2, top.shape[1]))], 0)


def turn_kernel(width, *refs):
    pieces, out = refs[:-1], refs[-1]
    rows = jnp.concatenate([p[...] for p in pieces], 0)
    count = rows.shape[0]
    tail = jnp.zeros((count, 2 * width - rows.shape[1]), bf16)
    out[:, :count] = rows[:, :width].T
    out[:, count:] = jnp.concatenate([rows[:, width:], tail], 1).T


def weights_kernel(distance, turned, e, dp, own, a, b, *outs):
    weights = outs[2]
    half, keys = outs[0].shape[1], weights.shape[1]
    count = e.shape[0]
    top, total, weighted = join(a[...], b[...], distance)
    factor = jnp.exp(own[0:1, :] - (top + jnp.log(total)))
    delta = weighted / total
    columns = []
    for t in range(0, factor.shape[1], 128):
        lanes = slice(t, t + 128)
        columns.append(jnp.concatenate([factor[:, lanes], jnp.broadcast_to(delta[:, lanes], (127, 128))], 0).T)
    pair = jnp.concatenate(columns, 0)[:count]
    probs = e[...] * pair[:, 0:1]
    dscores = probs * (dp[...] - pair[:, 1:2]) * score_scale
    both = jnp.concatenate([dscores.astype(bf16), probs.astype(bf16)], 0)
    weights[...] = both[:, :keys]
    for h in (0, 1):
        part = both[:, keys + h * half : keys + (h + 1) * half]
        outs[h][...] = jnp.dot(turned[...], part, preferred_element_type=f32).astype(bf16)


def grads_kernel(turned, weights, *outs):
    half = outs[0].shape[1]
    for h in (0, 1):
        outs[h][...] = jnp.dot(turned[...], weights[:, h * half : (h + 1) * half], preferred_element_type=f32)


def emit_kernel(left_a, left_b, right_a, right_b, kv, grad_out, input_out, grad, product, sems):
    half = left_a.shape[1]
    grad[:, :half] = left_a[...].astype(f32) + right_a[...].astype(f32)
    grad[:, half:] = left_b[...].astype(f32) + right_b[...].astype(f32)
    copies = [pltpu.make_async_copy(grad, grad_out, sems.at[0])]
    copies[0].start()
    left = grad[...].T.astype(bf16)
    total = kv.shape[1]
    step = 256 if total % 256 == 0 else total
    for i, c in enumerate(range(0, total, step)):
        cols = slice(c, c + step)
        product[:, cols] = jnp.dot(left, kv[:, cols], preferred_element_type=f32).astype(bf16)
        copy = pltpu.make_async_copy(product.at[:, cols], input_out.at[:, cols], sems.at[i + 1])
        copy.start()
        copies.append(copy)
    for copy in copies:
        copy.wait()


def kernel(body, results, operands, specs=None, out_specs=None, flops=0, **kw):
    moved = sum(a.size * a.dtype.itemsize for a in [*operands, *results])
    return pl.pallas_call(
        body,
        out_shape=results,
        in_specs=specs or [VMEM] * len(operands),
        out_specs=out_specs or (VMEM,) * len(results),
        compiler_params=pltpu.CompilerParams(vmem_limit_bytes=min(2 * moved + (4 << 20), 60 << 20)),
        cost_estimate=pl.CostEstimate(flops=flops, bytes_accessed=moved, transcendentals=0),
        **kw,
    )(*operands)


def shards(sizes, queries, query_pos, latents, valid_keys, output_gradient, kv_down):
    seq, head = sizes["seq"], sizes["head"]
    keys, width = latents.shape
    span = output_gradient.shape[2]
    model = kv_down.shape[0]
    heads = queries.shape[1]
    own_rows = queries.shape[0] * heads
    rows = own_rows * seq // 2
    lanes = -(-rows // 128) * 128
    half = keys // 2
    lat, kv = latents.T, kv_down.T
    here = lax.axis_index("seq").astype(jnp.int32).reshape(1)
    bits = bits_of(seq)
    pair, steps = bits[0], bits[:0:-1]

    own = jnp.concatenate([queries.reshape(own_rows, width), output_gradient.reshape(own_rows, span)], 1)
    pieces, offsets = gathered_rows(own, "seq", seq, steps)
    both, mask = kernel(
        functools.partial(prepare_kernel, offsets, own_rows, heads),
        (like((width, 2 * keys), bf16), like((rows, 2 * keys), f32)),
        (here, query_pos, valid_keys, swap(valid_keys, "seq", seq, pair), lat, swap(lat, "seq", seq, pair)),
        specs=[SMEM] * 4 + [VMEM] * 2,
        name="prepare",
    )
    e, dp, stats = kernel(
        functools.partial(scores_kernel, len(pieces)),
        (like((rows, 2 * keys), f32), like((rows, 2 * keys), f32), like((stat_rows, lanes), f32)),
        (*pieces, both, mask),
        flops=4 * rows * keys * (width + span),
        name="scores",
    )
    (turned,) = kernel(functools.partial(turn_kernel, width), (like((width, 2 * rows), bf16),), pieces, name="turn")

    joined = stats
    for i, bit in reversed(list(enumerate(steps))):
        other, distance = swap(joined, "seq", seq, bit), own_rows << i
        if i > 0:
            (joined,) = kernel(
                functools.partial(join_kernel, distance), (like(stats.shape, f32),), (joined, other), name="join"
            )

    *sent, weights = kernel(
        functools.partial(weights_kernel, distance),
        (like((width, half), bf16),) * 2 + (like((2 * rows, keys), bf16),),
        (turned, e, dp, stats, joined, other),
        flops=4 * rows * keys * width,
        name="weights",
    )
    received = [swap(g, "seq", seq, pair) for g in sent]
    halves = kernel(
        grads_kernel, (like((width, half), f32),) * 2, (turned, weights), flops=4 * rows * keys * width, name="grads"
    )
    halves = [(g + r.astype(f32)).astype(bf16) for g, r in zip(halves, received)]

    orders = (bits_of(head), bits_of(head)[::-1])
    for step in range(len(orders[0]) - 1):
        received = [swap(g, "head", head, order[step]) for g, order in zip(halves, orders)]
        halves = [(g.astype(f32) + r.astype(f32)).astype(bf16) for g, r in zip(halves, received)]
    received = [swap(g, "head", head, order[-1]) for g, order in zip(halves, orders)]

    latent_grad, input_grad = kernel(
        emit_kernel,
        (like((width, keys), f32), like((keys, model), bf16)),
        (*halves, *received, kv),
        out_specs=(HBM,) * 2,
        scratch_shapes=[
            pltpu.VMEM((width, keys), f32),
            pltpu.VMEM((keys, model), bf16),
            pltpu.SemaphoreType.DMA((1 + -(-model // 256),)),
        ],
        flops=2 * keys * width * model,
        name="emit",
    )
    return latent_grad.T, input_grad


def solution(mesh):
    placed = (
        P("seq", "head", None),
        P(),
        P("seq", None),
        P("seq"),
        P("seq", "head", None),
        P("head", None),
    )
    return jax.shard_map(
        functools.partial(shards, dict(mesh.shape)),
        mesh=mesh,
        in_specs=placed,
        out_specs=(P("seq", None), P("seq", "head")),
        check_vma=False,
    )
```

```python
import functools

import jax
import jax.numpy as jnp
from jax import lax
from jax.experimental import pallas as pl
from jax.experimental.pallas import tpu as pltpu
from jax.sharding import PartitionSpec as P

score_scale = 192.0 ** (-0.5)
hidden, shown = -1e30, 3e38
row_tile = 128
stat_rows, cap_rows = 8, 16
f32, bf16 = jnp.float32, jnp.bfloat16


VMEM = pl.BlockSpec(memory_space=pltpu.VMEM)
HBM = pl.BlockSpec(memory_space=pltpu.HBM)


def like(shape, dtype):
    return jax.ShapeDtypeStruct(shape, dtype)


def swap(value, axis, size, bits):
    return lax.ppermute(value, axis, [(i, i ^ bits) for i in range(size)])


def bits_of(size):
    assert size > 1 and size & (size - 1) == 0, "axis size"
    return [1 << i for i in range(size.bit_length() - 1)]


def partners(steps):
    for chosen in range(1, 1 << len(steps)):
        picked = [i for i in range(len(steps)) if chosen >> i & 1]
        yield sum(steps[i] for i in picked), picked


def gathered_rows(own, axis, size, steps):
    held = own
    for bits in steps[:-2]:
        held = jnp.concatenate([held, swap(held, axis, size, bits)], 0)
    return [held] + [swap(held, axis, size, bits) for bits, _ in partners(steps[-2:])]


def scores_kernel(n, width, span, *refs):
    pieces, (positions, own, other, e_out, dp_out, stats) = refs[:n], refs[n:]
    keys = own.shape[1]
    rows = jnp.concatenate([p[...] for p in pieces], 0)
    packs = []
    for t in range(0, rows.shape[0], row_tile):
        block = rows[t : t + row_tile]
        count = block.shape[0]
        index = lax.broadcasted_iota(jnp.int32, (count, keys), 1)
        scores, dps = [], []
        for part, lat in enumerate((own, other)):
            s = jnp.dot(block[:, span:], lat[:width, :], preferred_element_type=f32) * score_scale
            s = jnp.minimum(s, lat[width : width + 1, :].astype(f32))
            shard = lax.axis_index("seq") ^ part
            scores.append(jnp.where(index + shard * keys <= positions[t : t + count, :], s, hidden))
            dps.append(jnp.dot(block[:, :span], lat[:span, :], preferred_element_type=f32))
        s, dp = jnp.concatenate(scores, 1), jnp.concatenate(dps, 1)
        top = jnp.max(s, axis=1, keepdims=True)
        e = jnp.exp(s - top)
        e_out[t : t + count, :] = e
        dp_out[t : t + count, :] = dp
        total = jnp.sum(e, axis=1, keepdims=True)
        weighted = jnp.sum(e * dp, axis=1, keepdims=True)
        lane = lax.broadcasted_iota(jnp.int32, (count, 128), 1)
        packed = jnp.where(lane == 0, top, jnp.where(lane == 1, total, weighted))
        if count % 128:
            packed = jnp.concatenate([packed, jnp.zeros((128 - count % 128, 128), f32)], 0)
        packs.append(packed.T[:stat_rows, :])
    stats[...] = jnp.concatenate(packs, 1)


def aligned(b, distance):
    lanes = b.shape[1]
    lane = lax.broadcasted_iota(jnp.int32, b.shape, 1)
    return jnp.where((lane // distance) % 2 == 0, pltpu.roll(b, lanes - distance, 1), pltpu.roll(b, distance, 1))


def join(a, b):
    top = jnp.maximum(a[0:1], b[0:1])
    wa, wb = jnp.exp(a[0:1] - top), jnp.exp(b[0:1] - top)
    return jnp.concatenate([top, a[1:3] * wa + b[1:3] * wb], 0)


def join_kernel(distance, a, b, out):
    out[:3, :] = join(a[...], aligned(b[...], distance))


def turn_kernel(width, *refs):
    pieces, out = refs[:-1], refs[-1]
    rows = jnp.concatenate([p[...] for p in pieces], 0)
    count = rows.shape[0]
    tail = jnp.zeros((count, 2 * width - rows.shape[1]), bf16)
    span = rows.shape[1] - width
    out[:, :count] = rows[:, span:].T
    out[:, count:] = jnp.concatenate([rows[:, :span], tail], 1).T


def weights_kernel(distances, turned, e, dp, own, start, *refs):
    others, outs, weights = refs[:-3], refs[-3:-1], refs[-1]
    half, keys = outs[0].shape[1], weights.shape[1]
    count = e.shape[0]
    joined = start[...]
    for ref, pairs in zip(others, distances):
        other = ref[...]
        for distance in pairs:
            other = aligned(other, distance)
        joined = join(joined, other)
    factor = jnp.exp(own[0:1, :] - (joined[0:1] + jnp.log(joined[1:2])))
    delta = joined[2:3] / joined[1:2]
    columns = []
    for t in range(0, factor.shape[1], 128):
        lanes = slice(t, t + 128)
        columns.append(jnp.concatenate([factor[:, lanes], jnp.broadcast_to(delta[:, lanes], (127, 128))], 0).T)
    pair = jnp.concatenate(columns, 0)[:count]
    probs = e[...] * pair[:, 0:1]
    dscores = probs * (dp[...] - pair[:, 1:2]) * score_scale
    both = jnp.concatenate([dscores.astype(bf16), probs.astype(bf16)], 0)
    weights[...] = both[:, :keys]
    for h in (0, 1):
        part = both[:, keys + h * half : keys + (h + 1) * half]
        outs[h][...] = jnp.dot(turned[...], part, preferred_element_type=f32).astype(bf16)


def grads_kernel(turned, weights, *outs):
    half = outs[0].shape[1]
    for h in (0, 1):
        outs[h][...] = jnp.dot(turned[...], weights[:, h * half : (h + 1) * half], preferred_element_type=f32)


def emit_kernel(left_a, left_b, right_a, right_b, kv, grad_out, input_out, grad, product, sems):
    half = left_a.shape[1]
    grad[:, :half] = left_a[...].astype(f32) + right_a[...].astype(f32)
    grad[:, half:] = left_b[...].astype(f32) + right_b[...].astype(f32)
    copies = [pltpu.make_async_copy(grad, grad_out, sems.at[0])]
    copies[0].start()
    left = grad[...].T.astype(bf16)
    total = kv.shape[1]
    step = 256 if total % 256 == 0 else total
    for i, c in enumerate(range(0, total, step)):
        cols = slice(c, c + step)
        product[:, cols] = jnp.dot(left, kv[:, cols], preferred_element_type=f32).astype(bf16)
        copy = pltpu.make_async_copy(product.at[:, cols], input_out.at[:, cols], sems.at[i + 1])
        copy.start()
        copies.append(copy)
    for copy in copies:
        copy.wait()


def kernel(body, results, operands, specs=None, out_specs=None, flops=0, **kw):
    moved = sum(a.size * a.dtype.itemsize for a in [*operands, *results])
    return pl.pallas_call(
        body,
        out_shape=results,
        in_specs=specs or [VMEM] * len(operands),
        out_specs=out_specs or (VMEM,) * len(results),
        compiler_params=pltpu.CompilerParams(vmem_limit_bytes=min(2 * moved + (4 << 20), 60 << 20)),
        cost_estimate=pl.CostEstimate(flops=flops, bytes_accessed=moved, transcendentals=0),
        **kw,
    )(*operands)


def shards(sizes, queries, query_pos, latents, valid_keys, output_gradient, kv_down):
    seq, head = sizes["seq"], sizes["head"]
    keys, width = latents.shape
    span = output_gradient.shape[2]
    model = kv_down.shape[0]
    heads = queries.shape[1]
    own_rows = queries.shape[0] * heads
    rows = own_rows * seq // 2
    lanes = -(-rows // 128) * 128
    half = keys // 2
    lat, kv = latents.T, kv_down.T
    bits = bits_of(seq)
    pair, steps = bits[0], bits[:0:-1]

    own = jnp.concatenate([output_gradient.reshape(own_rows, span), queries.reshape(own_rows, width)], 1)
    pieces = gathered_rows(own, "seq", seq, steps)

    me = lax.axis_index("seq").astype(jnp.int32)
    caps = jnp.where(jnp.arange(keys, dtype=jnp.int32) < valid_keys[0], shown, hidden).astype(bf16)
    capped = jnp.concatenate([lat, jnp.broadcast_to(caps, (cap_rows, keys))], 0)
    with jax.named_scope("limits"):
        block = lax.broadcasted_iota(jnp.int32, (rows, query_pos.shape[0]), 0) // heads
        device = me ^ sum(((block // queries.shape[0] >> i) & 1) * bit for i, bit in enumerate(steps))
        query = device * queries.shape[0] + block % queries.shape[0]
        chosen = query == lax.broadcasted_iota(jnp.int32, query.shape, 1)
        position = jnp.max(jnp.where(chosen, query_pos, -1), 1, keepdims=True)

    e, dp, stats = kernel(
        functools.partial(scores_kernel, len(pieces), width, span),
        (like((rows, 2 * keys), f32), like((rows, 2 * keys), f32), like((stat_rows, lanes), f32)),
        (*pieces, position, capped, swap(capped, "seq", seq, pair)),
        flops=4 * rows * keys * (width + span),
        name="scores",
    )
    (turned,) = kernel(functools.partial(turn_kernel, width), (like((width, 2 * rows), bf16),), pieces, name="turn")

    joined, doubled = stats, max(0, len(steps) - 2)
    for i in range(doubled):
        (joined,) = kernel(
            functools.partial(join_kernel, own_rows << i),
            (like(stats.shape, f32),),
            (joined, swap(joined, "seq", seq, steps[i])),
            name="join",
        )
    direct = list(partners(steps[doubled:]))
    others = [swap(joined, "seq", seq, bits) for bits, _ in direct]
    distances = [[own_rows << doubled + i for i in picked] for _, picked in direct]

    *sent, weights = kernel(
        functools.partial(weights_kernel, distances),
        (like((width, half), bf16),) * 2 + (like((2 * rows, keys), bf16),),
        (turned, e, dp, stats, joined, *others),
        flops=4 * rows * keys * width,
        name="weights",
    )
    received = [swap(g, "seq", seq, pair) for g in sent]
    halves = kernel(
        grads_kernel, (like((width, half), f32),) * 2, (turned, weights), flops=4 * rows * keys * width, name="grads"
    )
    halves = [(g + r.astype(f32)).astype(bf16) for g, r in zip(halves, received)]

    orders = (bits_of(head), bits_of(head)[::-1])
    for step in range(len(orders[0]) - 1):
        received = [swap(g, "head", head, order[step]) for g, order in zip(halves, orders)]
        halves = [(g.astype(f32) + r.astype(f32)).astype(bf16) for g, r in zip(halves, received)]
    received = [swap(g, "head", head, order[-1]) for g, order in zip(halves, orders)]

    latent_grad, input_grad = kernel(
        emit_kernel,
        (like((width, keys), f32), like((keys, model), bf16)),
        (*halves, *received, kv),
        out_specs=(HBM,) * 2,
        scratch_shapes=[
            pltpu.VMEM((width, keys), f32),
            pltpu.VMEM((keys, model), bf16),
            pltpu.SemaphoreType.DMA((1 + -(-model // 256),)),
        ],
        flops=2 * keys * width * model,
        name="emit",
    )
    return latent_grad.T, input_grad


def solution(mesh):
    placed = (
        P("seq", "head", None),
        P(),
        P("seq", None),
        P("seq"),
        P("seq", "head", None),
        P("head", None),
    )
    return jax.shard_map(
        functools.partial(shards, dict(mesh.shape)),
        mesh=mesh,
        in_specs=placed,
        out_specs=(P("seq", None), P("seq", "head")),
        check_vma=False,
    )
```

```python
import functools

import jax
import jax.numpy as jnp
from jax import lax
from jax.experimental import pallas as pl
from jax.experimental.pallas import tpu as pltpu
from jax.sharding import PartitionSpec as P

score_scale = 192.0 ** (-0.5)
hidden, shown = -1e30, 3e38
row_tile = 256
spread_bytes = 16 << 20
stat_rows, cap_rows = 8, 16
f32, bf16 = jnp.float32, jnp.bfloat16


VMEM = pl.BlockSpec(memory_space=pltpu.VMEM)
HBM = pl.BlockSpec(memory_space=pltpu.HBM)


def like(shape, dtype):
    return jax.ShapeDtypeStruct(shape, dtype)


def swap(value, axis, size, bits):
    return lax.ppermute(value, axis, [(i, i ^ bits) for i in range(size)])


def bits_of(size):
    assert size > 1 and size & (size - 1) == 0, "axis size"
    return [1 << i for i in range(size.bit_length() - 1)]


def partners(steps):
    for chosen in range(1, 1 << len(steps)):
        picked = [i for i in range(len(steps)) if chosen >> i & 1]
        yield sum(steps[i] for i in picked), picked


def gathered_rows(own, axis, size, steps):
    held = own
    for bits in steps[:-2]:
        held = jnp.concatenate([held, swap(held, axis, size, bits)], 0)
    return [held] + [swap(held, axis, size, bits) for bits, _ in partners(steps[-2:])]


def merge_kernel(*refs):
    refs[-1][...] = jnp.concatenate([ref[...] for ref in refs[:-1]], 0)


def scores_kernel(width, span, *refs):
    rows, positions, own, other, e_out, dp_out, stats = refs
    keys = own.shape[1]
    packs = []
    for t in range(0, rows.shape[0], row_tile):
        block = rows[t : min(t + row_tile, rows.shape[0]), :]
        count = block.shape[0]
        index = lax.broadcasted_iota(jnp.int32, (count, keys), 1)
        scores, dps = [], []
        for part, lat in enumerate((own, other)):
            s = jnp.dot(block[:, span:], lat[:width, :], preferred_element_type=f32) * score_scale
            s = jnp.minimum(s, lat[width : width + 1, :].astype(f32))
            shard = lax.axis_index("seq") ^ part
            scores.append(jnp.where(index + shard * keys <= positions[t : t + count, :], s, hidden))
            dps.append(jnp.dot(block[:, :span], lat[:span, :], preferred_element_type=f32))
        s, dp = jnp.concatenate(scores, 1), jnp.concatenate(dps, 1)
        top = jnp.max(s, axis=1, keepdims=True)
        e = jnp.exp(s - top)
        e_out[t : t + count, :] = e
        dp_out[t : t + count, :] = dp
        total = jnp.sum(e, axis=1, keepdims=True)
        weighted = jnp.sum(e * dp, axis=1, keepdims=True)
        lane = lax.broadcasted_iota(jnp.int32, (count, 128), 1)
        packed = jnp.where(lane == 0, top, jnp.where(lane == 1, total, weighted))
        if count % 128:
            packed = jnp.concatenate([packed, jnp.zeros((128 - count % 128, 128), f32)], 0)
        packs.append(packed.T[:stat_rows, :])
    stats[...] = jnp.concatenate(packs, 1)


def aligned(b, distance):
    lanes = b.shape[1]
    lane = lax.broadcasted_iota(jnp.int32, b.shape, 1)
    return jnp.where((lane // distance) % 2 == 0, pltpu.roll(b, lanes - distance, 1), pltpu.roll(b, distance, 1))


def join(a, b):
    top = jnp.maximum(a[0:1], b[0:1])
    wa, wb = jnp.exp(a[0:1] - top), jnp.exp(b[0:1] - top)
    return jnp.concatenate([top, a[1:3] * wa + b[1:3] * wb], 0)


def join_kernel(distance, a, b, out):
    out[:3, :] = join(a[...], aligned(b[...], distance))


def turn_kernel(width, rows, out):
    count = rows.shape[0]
    span = rows.shape[1] - width
    tail = jnp.zeros((count, width - span), bf16)
    out[:, :count] = rows[:, span:].T
    out[:, count:] = jnp.concatenate([rows[:, :span], tail], 1).T


def weights_kernel(distances, turned, e, dp, own, start, *refs):
    others, outs, weights = refs[:-3], refs[-3:-1], refs[-1]
    half, keys = outs[0].shape[1], weights.shape[1]
    count = e.shape[0]
    joined = start[...]
    for ref, pairs in zip(others, distances):
        other = ref[...]
        for distance in pairs:
            other = aligned(other, distance)
        joined = join(joined, other)
    factor = jnp.exp(own[0:1, :] - (joined[0:1] + jnp.log(joined[1:2])))
    delta = joined[2:3] / joined[1:2]
    columns = []
    for t in range(0, factor.shape[1], 128):
        lanes = slice(t, t + 128)
        columns.append(jnp.concatenate([factor[:, lanes], jnp.broadcast_to(delta[:, lanes], (127, 128))], 0).T)
    pair = jnp.concatenate(columns, 0)[:count]
    probs = e[...] * pair[:, 0:1]
    dscores = probs * (dp[...] - pair[:, 1:2]) * score_scale
    both = jnp.concatenate([dscores.astype(bf16), probs.astype(bf16)], 0)
    weights[...] = both[:, :keys]
    for h in (0, 1):
        part = both[:, keys + h * half : keys + (h + 1) * half]
        outs[h][...] = jnp.dot(turned[...], part, preferred_element_type=f32).astype(bf16)


def grads_kernel(turned, weights, *outs):
    half = outs[0].shape[1]
    for h in (0, 1):
        outs[h][...] = jnp.dot(turned[...], weights[:, h * half : (h + 1) * half], preferred_element_type=f32)


def emit_kernel(left_a, left_b, right_a, right_b, kv, grad_out, input_out, grad, product, sems):
    half = left_a.shape[1]
    grad[:, :half] = left_a[...].astype(f32) + right_a[...].astype(f32)
    grad[:, half:] = left_b[...].astype(f32) + right_b[...].astype(f32)
    copies = [pltpu.make_async_copy(grad, grad_out, sems.at[0])]
    copies[0].start()
    left = grad[...].T.astype(bf16)
    total = kv.shape[1]
    step = 256 if total % 256 == 0 else total
    for i, c in enumerate(range(0, total, step)):
        cols = slice(c, c + step)
        product[:, cols] = jnp.dot(left, kv[:, cols], preferred_element_type=f32).astype(bf16)
        copy = pltpu.make_async_copy(product.at[:, cols], input_out.at[:, cols], sems.at[i + 1])
        copy.start()
        copies.append(copy)
    for copy in copies:
        copy.wait()


def kernel(body, results, operands, specs=None, out_specs=None, flops=0, **kw):
    moved = sum(a.size * a.dtype.itemsize for a in [*operands, *results])
    return pl.pallas_call(
        body,
        out_shape=results,
        in_specs=specs or [VMEM] * len(operands),
        out_specs=out_specs or (VMEM,) * len(results),
        compiler_params=pltpu.CompilerParams(vmem_limit_bytes=min(2 * moved + (4 << 20), 60 << 20)),
        cost_estimate=pl.CostEstimate(flops=flops, bytes_accessed=moved, transcendentals=0),
        **kw,
    )(*operands)


def shards(sizes, queries, query_pos, latents, valid_keys, output_gradient, kv_down):
    seq, head = sizes["seq"], sizes["head"]
    keys, width = latents.shape
    span = output_gradient.shape[2]
    model = kv_down.shape[0]
    heads = queries.shape[1]
    own_rows = queries.shape[0] * heads
    rows = own_rows * seq // 2
    half = keys // 2
    lat, kv = latents.T, kv_down.T
    bits = bits_of(seq)
    pair, steps = bits[0], bits[:0:-1]

    own = jnp.concatenate([output_gradient.reshape(own_rows, span), queries.reshape(own_rows, width)], 1)
    pieces = gathered_rows(own, "seq", seq, steps)
    (gathered,) = kernel(merge_kernel, (like((rows, span + width), bf16),), pieces, name="merge")
    spread = rows * head * 8 * (2 * keys + width) <= spread_bytes
    if spread:
        gathered, rows = lax.all_gather(gathered, "head", axis=0, tiled=True), rows * head
    lanes = -(-rows // 128) * 128

    me = lax.axis_index("seq").astype(jnp.int32)
    caps = jnp.where(jnp.arange(keys, dtype=jnp.int32) < valid_keys[0], shown, hidden).astype(bf16)
    capped = jnp.concatenate([lat, jnp.broadcast_to(caps, (cap_rows, keys))], 0)
    with jax.named_scope("limits"):
        block = lax.broadcasted_iota(jnp.int32, (rows, query_pos.shape[0]), 0) // heads
        device = me ^ sum(((block // queries.shape[0] >> i) & 1) * bit for i, bit in enumerate(steps))
        query = device * queries.shape[0] + block % queries.shape[0]
        chosen = query == lax.broadcasted_iota(jnp.int32, query.shape, 1)
        position = jnp.max(jnp.where(chosen, query_pos, -1), 1, keepdims=True)

    e, dp, stats = kernel(
        functools.partial(scores_kernel, width, span),
        (like((rows, 2 * keys), f32), like((rows, 2 * keys), f32), like((stat_rows, lanes), f32)),
        (gathered, position, capped, swap(capped, "seq", seq, pair)),
        flops=4 * rows * keys * (width + span),
        name="scores",
    )
    (turned,) = kernel(functools.partial(turn_kernel, width), (like((width, 2 * rows), bf16),), (gathered,), name="turn")

    joined, doubled = stats, max(0, len(steps) - 2)
    for i in range(doubled):
        (joined,) = kernel(
            functools.partial(join_kernel, own_rows << i),
            (like(stats.shape, f32),),
            (joined, swap(joined, "seq", seq, steps[i])),
            name="join",
        )
    direct = list(partners(steps[doubled:]))
    others = [swap(joined, "seq", seq, bits) for bits, _ in direct]
    distances = [[own_rows << doubled + i for i in picked] for _, picked in direct]

    *sent, weights = kernel(
        functools.partial(weights_kernel, distances),
        (like((width, half), bf16),) * 2 + (like((2 * rows, keys), bf16),),
        (turned, e, dp, stats, joined, *others),
        flops=4 * rows * keys * width,
        name="weights",
    )
    received = [swap(g, "seq", seq, pair) for g in sent]
    halves = kernel(
        grads_kernel, (like((width, half), f32),) * 2, (turned, weights), flops=4 * rows * keys * width, name="grads"
    )
    if not spread:
        halves = [(g + r.astype(f32)).astype(bf16) for g, r in zip(halves, received)]
        orders = (bits_of(head), bits_of(head)[::-1])
        for step in range(len(orders[0]) - 1):
            received = [swap(g, "head", head, order[step]) for g, order in zip(halves, orders)]
            halves = [(g.astype(f32) + r.astype(f32)).astype(bf16) for g, r in zip(halves, received)]
        received = [swap(g, "head", head, order[-1]) for g, order in zip(halves, orders)]

    latent_grad, input_grad = kernel(
        emit_kernel,
        (like((width, keys), f32), like((keys, model), bf16)),
        (*halves, *received, kv),
        out_specs=(HBM,) * 2,
        scratch_shapes=[
            pltpu.VMEM((width, keys), f32),
            pltpu.VMEM((keys, model), bf16),
            pltpu.SemaphoreType.DMA((1 + -(-model // 256),)),
        ],
        flops=2 * keys * width * model,
        name="emit",
    )
    return latent_grad.T, input_grad


def solution(mesh):
    placed = (
        P("seq", "head", None),
        P(),
        P("seq", None),
        P("seq"),
        P("seq", "head", None),
        P("head", None),
    )
    return jax.shard_map(
        functools.partial(shards, dict(mesh.shape)),
        mesh=mesh,
        in_specs=placed,
        out_specs=(P("seq", None), P("seq", "head")),
        check_vma=False,
    )
```

```python
import functools

import jax
import jax.numpy as jnp
from jax import lax
from jax.experimental import pallas as pl
from jax.experimental.pallas import tpu as pltpu
from jax.sharding import PartitionSpec as P

score_scale = 192.0 ** (-0.5)
hidden, shown = -1e30, 3e38
row_tile = 256
spread_bytes = 16 << 20
stat_rows, cap_rows = 8, 16
f32, bf16 = jnp.float32, jnp.bfloat16


VMEM = pl.BlockSpec(memory_space=pltpu.VMEM)
HBM = pl.BlockSpec(memory_space=pltpu.HBM)


def like(shape, dtype):
    return jax.ShapeDtypeStruct(shape, dtype)


def swap(value, axis, size, bits):
    return lax.ppermute(value, axis, [(i, i ^ bits) for i in range(size)])


def bits_of(size):
    assert size > 1 and size & (size - 1) == 0, "axis size"
    return [1 << i for i in range(size.bit_length() - 1)]


def partners(steps):
    for chosen in range(1, 1 << len(steps)):
        picked = [i for i in range(len(steps)) if chosen >> i & 1]
        yield sum(steps[i] for i in picked), picked


def gathered_rows(own, axis, size, steps):
    held = own
    for bits in steps[:-2]:
        held = jnp.concatenate([held, swap(held, axis, size, bits)], 0)
    return [held] + [swap(held, axis, size, bits) for bits, _ in partners(steps[-2:])]


def merge_kernel(*refs):
    refs[-1][...] = jnp.concatenate([ref[...] for ref in refs[:-1]], 0)


def scores_kernel(width, span, *refs):
    rows, positions, own, other, e_out, dp_out, stats = refs
    keys = own.shape[1]
    packs = []
    for t in range(0, rows.shape[0], row_tile):
        block = rows[t : min(t + row_tile, rows.shape[0]), :]
        count = block.shape[0]
        index = lax.broadcasted_iota(jnp.int32, (count, keys), 1)
        scores, dps = [], []
        for part, lat in enumerate((own, other)):
            s = jnp.dot(block[:, span:], lat[:width, :], preferred_element_type=f32) * score_scale
            s = jnp.minimum(s, lat[width : width + 1, :].astype(f32))
            shard = lax.axis_index("seq") ^ part
            scores.append(jnp.where(index + shard * keys <= positions[t : t + count, :], s, hidden))
            dps.append(jnp.dot(block[:, :span], lat[:span, :], preferred_element_type=f32))
        s, dp = jnp.concatenate(scores, 1), jnp.concatenate(dps, 1)
        top = jnp.max(s, axis=1, keepdims=True)
        e = jnp.exp(s - top)
        e_out[t : t + count, :] = e
        dp_out[t : t + count, :] = dp
        total = jnp.sum(e, axis=1, keepdims=True)
        weighted = jnp.sum(e * dp, axis=1, keepdims=True)
        lane = lax.broadcasted_iota(jnp.int32, (count, 128), 1)
        packed = jnp.where(lane == 0, top, jnp.where(lane == 1, total, weighted))
        if count % 128:
            packed = jnp.concatenate([packed, jnp.zeros((128 - count % 128, 128), f32)], 0)
        packs.append(packed.T[:stat_rows, :])
    stats[...] = jnp.concatenate(packs, 1)


def aligned(b, distance):
    lanes = b.shape[1]
    lane = lax.broadcasted_iota(jnp.int32, b.shape, 1)
    return jnp.where((lane // distance) % 2 == 0, pltpu.roll(b, lanes - distance, 1), pltpu.roll(b, distance, 1))


def join(a, b):
    top = jnp.maximum(a[0:1], b[0:1])
    wa, wb = jnp.exp(a[0:1] - top), jnp.exp(b[0:1] - top)
    return jnp.concatenate([top, a[1:3] * wa + b[1:3] * wb], 0)


def join_kernel(distances, start, *refs):
    joined = start[...]
    for ref, pairs in zip(refs[:-1], distances):
        other = ref[...]
        for distance in pairs:
            other = aligned(other, distance)
        joined = join(joined, other)
    refs[-1][:3, :] = joined


def turn_kernel(width, rows, out):
    count = rows.shape[0]
    span = rows.shape[1] - width
    tail = jnp.zeros((count, width - span), bf16)
    out[:, :count] = rows[:, span:].T
    out[:, count:] = jnp.concatenate([rows[:, :span], tail], 1).T


def grads_kernel(distance, first, turned, e, dp, own, start, last, out):
    count, keys = e.shape[0], slice(first, first + out.shape[1])
    joined = join(start[...], aligned(last[...], distance))
    factor = jnp.exp(own[0:1, :] - (joined[0:1] + jnp.log(joined[1:2])))
    delta = joined[2:3] / joined[1:2]
    columns = []
    for t in range(0, factor.shape[1], 128):
        lanes = slice(t, t + 128)
        columns.append(jnp.concatenate([factor[:, lanes], jnp.broadcast_to(delta[:, lanes], (127, 128))], 0).T)
    pair = jnp.concatenate(columns, 0)[:count]
    probs = e[:, keys] * pair[:, 0:1]
    dscores = probs * (dp[:, keys] - pair[:, 1:2]) * score_scale
    both = jnp.concatenate([dscores.astype(bf16), probs.astype(bf16)], 0)
    out[...] = jnp.dot(turned[...], both, preferred_element_type=f32).astype(out.dtype)


def emit_kernel(parts, *refs):
    left, right = refs[:parts], refs[parts : 2 * parts]
    kv, grad_out, input_out, grad, product, sems = refs[2 * parts :]
    at = 0
    for a, b in zip(left, right):
        grad[:, at : at + a.shape[1]] = a[...].astype(f32) + b[...].astype(f32)
        at += a.shape[1]
    copies = [pltpu.make_async_copy(grad, grad_out, sems.at[0])]
    copies[0].start()
    left = grad[...].astype(bf16).T
    total = kv.shape[1]
    step = 256 if total % 256 == 0 else total
    for i, c in enumerate(range(0, total, step)):
        cols = slice(c, c + step)
        product[:, cols] = jnp.dot(left, kv[:, cols], preferred_element_type=f32).astype(bf16)
        copy = pltpu.make_async_copy(product.at[:, cols], input_out.at[:, cols], sems.at[i + 1])
        copy.start()
        copies.append(copy)
    for copy in copies:
        copy.wait()


def kernel(body, results, operands, specs=None, out_specs=None, flops=0, **kw):
    moved = sum(a.size * a.dtype.itemsize for a in [*operands, *results])
    return pl.pallas_call(
        body,
        out_shape=results,
        in_specs=specs or [VMEM] * len(operands),
        out_specs=out_specs or (VMEM,) * len(results),
        compiler_params=pltpu.CompilerParams(vmem_limit_bytes=min(2 * moved + (4 << 20), 60 << 20)),
        cost_estimate=pl.CostEstimate(flops=flops, bytes_accessed=moved, transcendentals=0),
        **kw,
    )(*operands)


def shards(sizes, queries, query_pos, latents, valid_keys, output_gradient, kv_down):
    seq, head = sizes["seq"], sizes["head"]
    keys, width = latents.shape
    span = output_gradient.shape[2]
    model = kv_down.shape[0]
    heads = queries.shape[1]
    own_rows = queries.shape[0] * heads
    rows = own_rows * seq // 2
    lat, kv = latents.T, kv_down.T
    bits = bits_of(seq)
    pair, steps = bits[0], bits[:0:-1]

    own = jnp.concatenate([output_gradient.reshape(own_rows, span), queries.reshape(own_rows, width)], 1)
    pieces = gathered_rows(own, "seq", seq, steps)
    (gathered,) = kernel(merge_kernel, (like((rows, span + width), bf16),), pieces, name="merge")
    spread = rows * head * 8 * (2 * keys + width) <= spread_bytes
    if spread:
        gathered, rows = lax.all_gather(gathered, "head", axis=0, tiled=True), rows * head
    lanes = -(-rows // 128) * 128

    me = lax.axis_index("seq").astype(jnp.int32)
    caps = jnp.where(jnp.arange(keys, dtype=jnp.int32) < valid_keys[0], shown, hidden).astype(bf16)
    capped = jnp.concatenate([lat, jnp.broadcast_to(caps, (cap_rows, keys))], 0)
    with jax.named_scope("limits"):
        block = lax.broadcasted_iota(jnp.int32, (rows, query_pos.shape[0]), 0) // heads
        device = me ^ sum(((block // queries.shape[0] >> i) & 1) * bit for i, bit in enumerate(steps))
        query = device * queries.shape[0] + block % queries.shape[0]
        chosen = query == lax.broadcasted_iota(jnp.int32, query.shape, 1)
        position = jnp.max(jnp.where(chosen, query_pos, -1), 1, keepdims=True)

    e, dp, stats = kernel(
        functools.partial(scores_kernel, width, span),
        (like((rows, 2 * keys), f32), like((rows, 2 * keys), f32), like((stat_rows, lanes), f32)),
        (gathered, position, capped, swap(capped, "seq", seq, pair)),
        flops=4 * rows * keys * (width + span),
        name="scores",
    )
    (turned,) = kernel(functools.partial(turn_kernel, width), (like((width, 2 * rows), bf16),), (gathered,), name="turn")

    joined, doubled = stats, max(0, len(steps) - 2)
    for i in range(doubled):
        (joined,) = kernel(
            functools.partial(join_kernel, [[own_rows << i]]),
            (like(stats.shape, f32),),
            (joined, swap(joined, "seq", seq, steps[i])),
            name="join",
        )
    (bits, last), *direct = partners(steps[doubled:])
    others = [swap(joined, "seq", seq, bits)] + [swap(joined, "seq", seq, bits) for bits, _ in direct]
    if direct:
        distances = [[own_rows << doubled + i for i in picked] for _, picked in direct]
        (joined,) = kernel(
            functools.partial(join_kernel, distances), (like(stats.shape, f32),), (joined, *others[1:]), name="join"
        )

    def grads(first, dtype, name):
        return kernel(
            functools.partial(grads_kernel, own_rows << doubled + last[0], first),
            (like((width, keys), dtype),),
            (turned, e, dp, stats, joined, others[0]),
            flops=4 * rows * keys * width,
            name=name,
        )[0]

    received = swap(grads(keys, bf16, "grads_other"), "seq", seq, pair)
    mine = grads(0, f32, "grads_own")
    left, right = [mine], [received]
    if not spread:
        whole = (mine + received.astype(f32)).astype(bf16)
        left = [whole[:, : keys // 2], whole[:, keys // 2 :]]
        orders = (bits_of(head), bits_of(head)[::-1])
        for step in range(len(orders[0])):
            right = [swap(g, "head", head, order[step]) for g, order in zip(left, orders)]
            if step < len(orders[0]) - 1:
                left = [(g.astype(f32) + r.astype(f32)).astype(bf16) for g, r in zip(left, right)]

    latent_grad, input_grad = kernel(
        functools.partial(emit_kernel, len(left)),
        (like((width, keys), f32), like((keys, model), bf16)),
        (*left, *right, kv),
        out_specs=(HBM,) * 2,
        scratch_shapes=[
            pltpu.VMEM((width, keys), f32),
            pltpu.VMEM((keys, model), bf16),
            pltpu.SemaphoreType.DMA((1 + -(-model // 256),)),
        ],
        flops=2 * keys * width * model,
        name="emit",
    )
    return latent_grad.T, input_grad


def solution(mesh):
    placed = (
        P("seq", "head", None),
        P(),
        P("seq", None),
        P("seq"),
        P("seq", "head", None),
        P("head", None),
    )
    return jax.shard_map(
        functools.partial(shards, dict(mesh.shape)),
        mesh=mesh,
        in_specs=placed,
        out_specs=(P("seq", None), P("seq", "head")),
        check_vma=False,
    )
```

```python
import functools

import jax
import jax.numpy as jnp
from jax import lax
from jax.experimental import pallas as pl
from jax.experimental.pallas import tpu as pltpu
from jax.sharding import PartitionSpec as P

score_scale = 192.0 ** (-0.5)
hidden, shown = -1e30, 3e38
row_tile = 256
spread_bytes = 16 << 20
stat_rows, cap_rows = 8, 16
f32, bf16 = jnp.float32, jnp.bfloat16


VMEM = pl.BlockSpec(memory_space=pltpu.VMEM)
HBM = pl.BlockSpec(memory_space=pltpu.HBM)


def like(shape, dtype):
    return jax.ShapeDtypeStruct(shape, dtype)


def swap(value, axis, size, bits):
    return lax.ppermute(value, axis, [(i, i ^ bits) for i in range(size)])


def bits_of(size):
    assert size > 1 and size & (size - 1) == 0, "axis size"
    return [1 << i for i in range(size.bit_length() - 1)]


def partners(steps):
    for chosen in range(1, 1 << len(steps)):
        picked = [i for i in range(len(steps)) if chosen >> i & 1]
        yield sum(steps[i] for i in picked), picked


def gathered_rows(own, axis, size, steps):
    held = own
    for bits in steps[:-2]:
        held = jnp.concatenate([held, swap(held, axis, size, bits)], 0)
    listed = [bits for bits, _ in partners(steps[-2:])]
    made = {i: swap(held, axis, size, listed[i]) for i in reversed(range(len(listed)))}
    return [held] + [made[i] for i in range(len(listed))]


def tight_kernel(*refs):
    rows, out = jnp.concatenate([ref[...] for ref in refs[:-1]], 0), refs[-1]
    count, whole = rows.shape[0], rows.shape[1] // 128
    for t in range(whole):
        out[t * count : (t + 1) * count, :] = rows[:, t * 128 : (t + 1) * 128]
    end = rows[:, whole * 128 :]
    out[whole * count :, :] = jnp.concatenate([end[: count // 2], end[count // 2 :]], 1)


def loose_kernel(groups, tight, out):
    count, whole, length = out.shape[0] // groups, out.shape[1] // 128, tight.shape[0] // groups
    for g in range(groups):
        at, rows = g * length, slice(g * count, (g + 1) * count)
        for t in range(whole):
            out[rows, t * 128 : (t + 1) * 128] = tight[at + t * count : at + (t + 1) * count, :]
        end = tight[at + whole * count : at + length, :]
        out[rows, whole * 128 :] = jnp.concatenate([end[:, :64], end[:, 64:]], 0)


def merge_kernel(*refs):
    refs[-1][...] = jnp.concatenate([ref[...] for ref in refs[:-1]], 0)


def scores_kernel(width, span, *refs):
    rows, positions, own, other, e_out, dp_out, stats = refs
    keys = own.shape[1]
    packs = []
    for t in range(0, rows.shape[0], row_tile):
        block = rows[t : min(t + row_tile, rows.shape[0]), :]
        count = block.shape[0]
        index = lax.broadcasted_iota(jnp.int32, (count, keys), 1)
        scores, dps = [], []
        for part, lat in enumerate((own, other)):
            s = jnp.dot(block[:, span:], lat[:width, :], preferred_element_type=f32) * score_scale
            s = jnp.minimum(s, lat[width : width + 1, :].astype(f32))
            shard = lax.axis_index("seq") ^ part
            scores.append(jnp.where(index + shard * keys <= positions[t : t + count, :], s, hidden))
            dps.append(jnp.dot(block[:, :span], lat[:span, :], preferred_element_type=f32))
        s, dp = jnp.concatenate(scores, 1), jnp.concatenate(dps, 1)
        top = jnp.max(s, axis=1, keepdims=True)
        e = jnp.exp(s - top)
        e_out[t : t + count, :] = e
        dp_out[t : t + count, :] = dp
        total = jnp.sum(e, axis=1, keepdims=True)
        weighted = jnp.sum(e * dp, axis=1, keepdims=True)
        lane = lax.broadcasted_iota(jnp.int32, (count, 128), 1)
        packed = jnp.where(lane == 0, top, jnp.where(lane == 1, total, weighted))
        if count % 128:
            packed = jnp.concatenate([packed, jnp.zeros((128 - count % 128, 128), f32)], 0)
        packs.append(packed.T[:stat_rows, :])
    stats[...] = jnp.concatenate(packs, 1)


def aligned(b, distance):
    lanes = b.shape[1]
    lane = lax.broadcasted_iota(jnp.int32, b.shape, 1)
    return jnp.where((lane // distance) % 2 == 0, pltpu.roll(b, lanes - distance, 1), pltpu.roll(b, distance, 1))


def join(a, b):
    top = jnp.maximum(a[0:1], b[0:1])
    wa, wb = jnp.exp(a[0:1] - top), jnp.exp(b[0:1] - top)
    return jnp.concatenate([top, a[1:3] * wa + b[1:3] * wb], 0)


def join_kernel(distances, start, *refs):
    joined = start[...]
    for ref, pairs in zip(refs[:-1], distances):
        other = ref[...]
        for distance in pairs:
            other = aligned(other, distance)
        joined = join(joined, other)
    refs[-1][:3, :] = joined


def turn_kernel(width, rows, out):
    count = rows.shape[0]
    span = rows.shape[1] - width
    tail = jnp.zeros((count, width - span), bf16)
    out[:, :count] = rows[:, span:].T
    out[:, count:] = jnp.concatenate([rows[:, :span], tail], 1).T


def grads_kernel(distance, first, turned, e, dp, own, start, last, out):
    count, keys = e.shape[0], slice(first, first + out.shape[1])
    joined = join(start[...], aligned(last[...], distance))
    factor = jnp.exp(own[0:1, :] - (joined[0:1] + jnp.log(joined[1:2])))
    delta = joined[2:3] / joined[1:2]
    columns = []
    for t in range(0, factor.shape[1], 128):
        lanes = slice(t, t + 128)
        columns.append(jnp.concatenate([factor[:, lanes], jnp.broadcast_to(delta[:, lanes], (127, 128))], 0).T)
    pair = jnp.concatenate(columns, 0)[:count]
    probs = e[:, keys] * pair[:, 0:1]
    dscores = probs * (dp[:, keys] - pair[:, 1:2])
    value = jnp.dot(turned[:, count:], probs.astype(bf16), preferred_element_type=f32)
    key = jnp.dot(turned[:, :count], dscores.astype(bf16), preferred_element_type=f32)
    out[...] = (key * score_scale + value).astype(out.dtype)


def emit_kernel(parts, *refs):
    left, right = refs[:parts], refs[parts : 2 * parts]
    kv, grad_out, input_out, grad, product, sems = refs[2 * parts :]
    at = 0
    for a, b in zip(left, right):
        grad[:, at : at + a.shape[1]] = a[...].astype(f32) + b[...].astype(f32)
        at += a.shape[1]
    copies = [pltpu.make_async_copy(grad, grad_out, sems.at[0])]
    copies[0].start()
    left = grad[...].astype(bf16).T
    total = kv.shape[1]
    step = 256 if total % 256 == 0 else total
    for i, c in enumerate(range(0, total, step)):
        cols = slice(c, c + step)
        product[:, cols] = jnp.dot(left, kv[:, cols], preferred_element_type=f32).astype(bf16)
        copy = pltpu.make_async_copy(product.at[:, cols], input_out.at[:, cols], sems.at[i + 1])
        copy.start()
        copies.append(copy)
    for copy in copies:
        copy.wait()


def kernel(body, results, operands, specs=None, out_specs=None, flops=0, **kw):
    moved = sum(a.size * a.dtype.itemsize for a in [*operands, *results])
    return pl.pallas_call(
        body,
        out_shape=results,
        in_specs=specs or [VMEM] * len(operands),
        out_specs=out_specs or (VMEM,) * len(results),
        compiler_params=pltpu.CompilerParams(vmem_limit_bytes=min(2 * moved + (4 << 20), 60 << 20)),
        cost_estimate=pl.CostEstimate(flops=flops, bytes_accessed=moved, transcendentals=0),
        **kw,
    )(*operands)


def shards(sizes, queries, query_pos, latents, valid_keys, output_gradient, kv_down):
    seq, head = sizes["seq"], sizes["head"]
    keys, width = latents.shape
    span = output_gradient.shape[2]
    model = kv_down.shape[0]
    heads = queries.shape[1]
    own_rows = queries.shape[0] * heads
    rows = own_rows * seq // 2
    lat, kv = latents.T, kv_down.T
    bits = bits_of(seq)
    pair, steps = bits[0], bits[:0:-1]

    own = jnp.concatenate([output_gradient.reshape(own_rows, span), queries.reshape(own_rows, width)], 1)
    pieces = gathered_rows(own, "seq", seq, steps)
    spread = rows * head * 8 * (2 * keys + width) <= spread_bytes
    columns = span + width
    if spread and columns % 128 == 64 and rows % 32 == 0:
        shape = (rows * columns // 128, 128)
        (gathered,) = kernel(tight_kernel, (like(shape, bf16),), pieces, name="tight")
        gathered, rows = lax.all_gather(gathered, "head", axis=0, tiled=True), rows * head
        (gathered,) = kernel(
            functools.partial(loose_kernel, head), (like((rows, columns), bf16),), (gathered,), name="loose"
        )
    else:
        (gathered,) = kernel(merge_kernel, (like((rows, columns), bf16),), pieces, name="merge")
        if spread:
            gathered, rows = lax.all_gather(gathered, "head", axis=0, tiled=True), rows * head
    lanes = -(-rows // 128) * 128

    me = lax.axis_index("seq").astype(jnp.int32)
    caps = jnp.where(jnp.arange(keys, dtype=jnp.int32) < valid_keys[0], shown, hidden).astype(bf16)
    capped = jnp.concatenate([lat, jnp.broadcast_to(caps, (cap_rows, keys))], 0)
    with jax.named_scope("limits"):
        block = lax.broadcasted_iota(jnp.int32, (rows, query_pos.shape[0]), 0) // heads
        device = me ^ sum(((block // queries.shape[0] >> i) & 1) * bit for i, bit in enumerate(steps))
        query = device * queries.shape[0] + block % queries.shape[0]
        chosen = query == lax.broadcasted_iota(jnp.int32, query.shape, 1)
        position = jnp.max(jnp.where(chosen, query_pos, -1), 1, keepdims=True)

    e, dp, stats = kernel(
        functools.partial(scores_kernel, width, span),
        (like((rows, 2 * keys), f32), like((rows, 2 * keys), f32), like((stat_rows, lanes), f32)),
        (gathered, position, capped, swap(capped, "seq", seq, pair)),
        flops=4 * rows * keys * (width + span),
        name="scores",
    )
    (turned,) = kernel(functools.partial(turn_kernel, width), (like((width, 2 * rows), bf16),), (gathered,), name="turn")

    joined, doubled = stats, max(0, len(steps) - 2)
    for i in range(doubled):
        (joined,) = kernel(
            functools.partial(join_kernel, [[own_rows << i]]),
            (like(stats.shape, f32),),
            (joined, swap(joined, "seq", seq, steps[i])),
            name="join",
        )
    (bits, last), *direct = partners(steps[doubled:])
    others = [swap(joined, "seq", seq, bits)] + [swap(joined, "seq", seq, bits) for bits, _ in direct]
    if direct:
        distances = [[own_rows << doubled + i for i in picked] for _, picked in direct]
        (joined,) = kernel(
            functools.partial(join_kernel, distances), (like(stats.shape, f32),), (joined, *others[1:]), name="join"
        )

    def grads(first, dtype, name):
        return kernel(
            functools.partial(grads_kernel, own_rows << doubled + last[0], first),
            (like((width, keys), dtype),),
            (turned, e, dp, stats, joined, others[0]),
            flops=4 * rows * keys * width,
            name=name,
        )[0]

    received = swap(grads(keys, bf16, "grads_other"), "seq", seq, pair)
    mine = grads(0, f32, "grads_own")
    left, right = [mine], [received]
    if not spread:
        whole = (mine + received.astype(f32)).astype(bf16)
        left = [whole[:, : keys // 2], whole[:, keys // 2 :]]
        orders = (bits_of(head), bits_of(head)[::-1])
        for step in range(len(orders[0])):
            right = [swap(g, "head", head, order[step]) for g, order in zip(left, orders)]
            if step < len(orders[0]) - 1:
                left = [(g.astype(f32) + r.astype(f32)).astype(bf16) for g, r in zip(left, right)]

    latent_grad, input_grad = kernel(
        functools.partial(emit_kernel, len(left)),
        (like((width, keys), f32), like((keys, model), bf16)),
        (*left, *right, kv),
        out_specs=(HBM,) * 2,
        scratch_shapes=[
            pltpu.VMEM((width, keys), f32),
            pltpu.VMEM((keys, model), bf16),
            pltpu.SemaphoreType.DMA((1 + -(-model // 256),)),
        ],
        flops=2 * keys * width * model,
        name="emit",
    )
    return latent_grad.T, input_grad


def solution(mesh):
    placed = (
        P("seq", "head", None),
        P(),
        P("seq", None),
        P("seq"),
        P("seq", "head", None),
        P("head", None),
    )
    return jax.shard_map(
        functools.partial(shards, dict(mesh.shape)),
        mesh=mesh,
        in_specs=placed,
        out_specs=(P("seq", None), P("seq", "head")),
        check_vma=False,
    )
```

```python
import functools

import jax
import jax.numpy as jnp
from jax import lax
from jax.experimental import pallas as pl
from jax.experimental.pallas import tpu as pltpu
from jax.sharding import PartitionSpec as P

score_scale = 192.0 ** (-0.5)
hidden, shown = -1e30, 3e38
row_tile = 256
spread_bytes = 16 << 20
stat_rows, cap_rows = 8, 16
f32, bf16 = jnp.float32, jnp.bfloat16


VMEM = pl.BlockSpec(memory_space=pltpu.VMEM)
HBM = pl.BlockSpec(memory_space=pltpu.HBM)


def like(shape, dtype):
    return jax.ShapeDtypeStruct(shape, dtype)


def swap(value, axis, size, bits):
    return lax.ppermute(value, axis, [(i, i ^ bits) for i in range(size)])


def bits_of(size):
    assert size > 1 and size & (size - 1) == 0, "axis size"
    return [1 << i for i in range(size.bit_length() - 1)]


def partners(steps):
    for chosen in range(1, 1 << len(steps)):
        picked = [i for i in range(len(steps)) if chosen >> i & 1]
        yield sum(steps[i] for i in picked), picked


def gathered_rows(own, axis, size, steps):
    held = own
    for bits in steps[:-2]:
        held = jnp.concatenate([held, swap(held, axis, size, bits)], 0)
    return [held] + [swap(held, axis, size, bits) for bits, _ in partners(steps[-2:])]


def merge_kernel(*refs):
    refs[-1][...] = jnp.concatenate([ref[...] for ref in refs[:-1]], 0)


def scores_kernel(width, span, *refs):
    rows, positions, own, other, e_out, dp_out, stats = refs
    keys = own.shape[1]
    packs = []
    for t in range(0, rows.shape[0], row_tile):
        block = rows[t : min(t + row_tile, rows.shape[0]), :]
        count = block.shape[0]
        index = lax.broadcasted_iota(jnp.int32, (count, keys), 1)
        scores, dps = [], []
        for part, lat in enumerate((own, other)):
            s = jnp.dot(block[:, span:], lat[:width, :], preferred_element_type=f32) * score_scale
            s = jnp.minimum(s, lat[width : width + 1, :].astype(f32))
            shard = lax.axis_index("seq") ^ part
            scores.append(jnp.where(index + shard * keys <= positions[t : t + count, :], s, hidden))
            dps.append(jnp.dot(block[:, :span], lat[:span, :], preferred_element_type=f32))
        s, dp = jnp.concatenate(scores, 1), jnp.concatenate(dps, 1)
        top = jnp.max(s, axis=1, keepdims=True)
        e = jnp.exp(s - top)
        e_out[t : t + count, :] = e
        dp_out[t : t + count, :] = dp
        total = jnp.sum(e, axis=1, keepdims=True)
        weighted = jnp.sum(e * dp, axis=1, keepdims=True)
        lane = lax.broadcasted_iota(jnp.int32, (count, 128), 1)
        packed = jnp.where(lane == 0, top, jnp.where(lane == 1, total, weighted))
        if count % 128:
            packed = jnp.concatenate([packed, jnp.zeros((128 - count % 128, 128), f32)], 0)
        packs.append(packed.T[:stat_rows, :])
    stats[...] = jnp.concatenate(packs, 1)


def aligned(b, distance):
    lanes = b.shape[1]
    lane = lax.broadcasted_iota(jnp.int32, b.shape, 1)
    return jnp.where((lane // distance) % 2 == 0, pltpu.roll(b, lanes - distance, 1), pltpu.roll(b, distance, 1))


def join(a, b):
    top = jnp.maximum(a[0:1], b[0:1])
    wa, wb = jnp.exp(a[0:1] - top), jnp.exp(b[0:1] - top)
    return jnp.concatenate([top, a[1:3] * wa + b[1:3] * wb], 0)


def join_kernel(distances, start, *refs):
    joined = start[...]
    for ref, pairs in zip(refs[:-1], distances):
        other = ref[...]
        for distance in pairs:
            other = aligned(other, distance)
        joined = join(joined, other)
    refs[-1][:3, :] = joined


def turn_kernel(width, rows, out):
    count = rows.shape[0]
    span = rows.shape[1] - width
    tail = jnp.zeros((count, width - span), bf16)
    out[:, :count] = rows[:, span:].T
    out[:, count:] = jnp.concatenate([rows[:, :span], tail], 1).T


def grads_kernel(distance, first, turned, e, dp, own, start, last, out):
    count, keys = e.shape[0], slice(first, first + out.shape[1])
    joined = join(start[...], aligned(last[...], distance))
    factor = jnp.exp(own[0:1, :] - (joined[0:1] + jnp.log(joined[1:2])))
    delta = joined[2:3] / joined[1:2]
    columns = []
    for t in range(0, factor.shape[1], 128):
        lanes = slice(t, t + 128)
        columns.append(jnp.concatenate([factor[:, lanes], jnp.broadcast_to(delta[:, lanes], (127, 128))], 0).T)
    pair = jnp.concatenate(columns, 0)[:count]
    probs = e[:, keys] * pair[:, 0:1]
    dscores = probs * (dp[:, keys] - pair[:, 1:2])
    value = jnp.dot(turned[:, count:], probs.astype(bf16), preferred_element_type=f32)
    key = jnp.dot(turned[:, :count], dscores.astype(bf16), preferred_element_type=f32)
    out[...] = (key * score_scale + value).astype(out.dtype)


def emit_kernel(parts, *refs):
    left, right = refs[:parts], refs[parts : 2 * parts]
    kv, grad_out, input_out, grad, product, sems = refs[2 * parts :]
    at = 0
    for a, b in zip(left, right):
        grad[:, at : at + a.shape[1]] = a[...].astype(f32) + b[...].astype(f32)
        at += a.shape[1]
    copies = [pltpu.make_async_copy(grad, grad_out, sems.at[0])]
    copies[0].start()
    left = grad[...].astype(bf16).T
    total = kv.shape[1]
    step = 256 if total % 256 == 0 else total
    for i, c in enumerate(range(0, total, step)):
        cols = slice(c, c + step)
        product[:, cols] = jnp.dot(left, kv[:, cols], preferred_element_type=f32).astype(bf16)
        copy = pltpu.make_async_copy(product.at[:, cols], input_out.at[:, cols], sems.at[i + 1])
        copy.start()
        copies.append(copy)
    for copy in copies:
        copy.wait()


def kernel(body, results, operands, specs=None, out_specs=None, flops=0, **kw):
    moved = sum(a.size * a.dtype.itemsize for a in [*operands, *results])
    return pl.pallas_call(
        body,
        out_shape=results,
        in_specs=specs or [VMEM] * len(operands),
        out_specs=out_specs or (VMEM,) * len(results),
        compiler_params=pltpu.CompilerParams(vmem_limit_bytes=min(2 * moved + (4 << 20), 60 << 20)),
        cost_estimate=pl.CostEstimate(flops=flops, bytes_accessed=moved, transcendentals=0),
        **kw,
    )(*operands)


def shards(sizes, queries, query_pos, latents, valid_keys, output_gradient, kv_down):
    seq, head = sizes["seq"], sizes["head"]
    keys, width = latents.shape
    span = output_gradient.shape[2]
    model = kv_down.shape[0]
    heads = queries.shape[1]
    own_rows = queries.shape[0] * heads
    rows = own_rows * seq // 2
    lat, kv = latents.T, kv_down.T
    bits = bits_of(seq)
    pair, steps = bits[0], bits[:0:-1]

    own = jnp.concatenate([output_gradient.reshape(own_rows, span), queries.reshape(own_rows, width)], 1)
    pieces = gathered_rows(own, "seq", seq, steps)
    (gathered,) = kernel(merge_kernel, (like((rows, span + width), bf16),), pieces, name="merge")
    spread = rows * head * 8 * (2 * keys + width) <= spread_bytes
    if spread:
        gathered, rows = lax.all_gather(gathered, "head", axis=0, tiled=True), rows * head
    lanes = -(-rows // 128) * 128

    me = lax.axis_index("seq").astype(jnp.int32)
    caps = jnp.where(jnp.arange(keys, dtype=jnp.int32) < valid_keys[0], shown, hidden).astype(bf16)
    capped = jnp.concatenate([lat, jnp.broadcast_to(caps, (cap_rows, keys))], 0)
    with jax.named_scope("limits"):
        block = lax.broadcasted_iota(jnp.int32, (rows, query_pos.shape[0]), 0) // heads
        device = me ^ sum(((block // queries.shape[0] >> i) & 1) * bit for i, bit in enumerate(steps))
        query = device * queries.shape[0] + block % queries.shape[0]
        chosen = query == lax.broadcasted_iota(jnp.int32, query.shape, 1)
        position = jnp.max(jnp.where(chosen, query_pos, -1), 1, keepdims=True)

    e, dp, stats = kernel(
        functools.partial(scores_kernel, width, span),
        (like((rows, 2 * keys), f32), like((rows, 2 * keys), f32), like((stat_rows, lanes), f32)),
        (gathered, position, capped, swap(capped, "seq", seq, pair)),
        flops=4 * rows * keys * (width + span),
        name="scores",
    )
    (turned,) = kernel(functools.partial(turn_kernel, width), (like((width, 2 * rows), bf16),), (gathered,), name="turn")

    joined, doubled = stats, max(0, len(steps) - 2)
    for i in range(doubled):
        (joined,) = kernel(
            functools.partial(join_kernel, [[own_rows << i]]),
            (like(stats.shape, f32),),
            (joined, swap(joined, "seq", seq, steps[i])),
            name="join",
        )
    (bits, last), *direct = partners(steps[doubled:])
    others = [swap(joined, "seq", seq, bits)] + [swap(joined, "seq", seq, bits) for bits, _ in direct]
    if direct:
        distances = [[own_rows << doubled + i for i in picked] for _, picked in direct]
        (joined,) = kernel(
            functools.partial(join_kernel, distances), (like(stats.shape, f32),), (joined, *others[1:]), name="join"
        )

    def grads(first, dtype, name):
        return kernel(
            functools.partial(grads_kernel, own_rows << doubled + last[0], first),
            (like((width, keys), dtype),),
            (turned, e, dp, stats, joined, others[0]),
            flops=4 * rows * keys * width,
            name=name,
        )[0]

    received = swap(grads(keys, bf16, "grads_other"), "seq", seq, pair)
    mine = grads(0, f32, "grads_own")
    left, right = [mine], [received]
    if not spread:
        whole = (mine + received.astype(f32)).astype(bf16)
        left = [whole[:, : keys // 2], whole[:, keys // 2 :]]
        orders = (bits_of(head), bits_of(head)[::-1])
        for step in range(len(orders[0])):
            right = [swap(g, "head", head, order[step]) for g, order in zip(left, orders)]
            if step < len(orders[0]) - 1:
                left = [(g.astype(f32) + r.astype(f32)).astype(bf16) for g, r in zip(left, right)]

    latent_grad, input_grad = kernel(
        functools.partial(emit_kernel, len(left)),
        (like((width, keys), f32), like((keys, model), bf16)),
        (*left, *right, kv),
        out_specs=(HBM,) * 2,
        scratch_shapes=[
            pltpu.VMEM((width, keys), f32),
            pltpu.VMEM((keys, model), bf16),
            pltpu.SemaphoreType.DMA((1 + -(-model // 256),)),
        ],
        flops=2 * keys * width * model,
        name="emit",
    )
    return latent_grad.T, input_grad


def solution(mesh):
    placed = (
        P("seq", "head", None),
        P(),
        P("seq", None),
        P("seq"),
        P("seq", "head", None),
        P("head", None),
    )
    return jax.shard_map(
        functools.partial(shards, dict(mesh.shape)),
        mesh=mesh,
        in_specs=placed,
        out_specs=(P("seq", None), P("seq", "head")),
        check_vma=False,
    )
```
